32 devices in a mesh: dp: 2 (over x), head: 16 (over z, y, core).
Axes of the slice: x: 2, y: 2, z: 4, core: 2. Of those that a mesh axis runs over, the one named last changes fastest.
Arguments:
- queries: bfloat16 [2048, 8192], P('dp', 'head'), may hold values from -14 to 14
- keys: bfloat16 [2048, 8192], P('dp', 'head'), may hold values from -14 to 14
- values: bfloat16 [2048, 8192], P('dp', 'head'), may hold values from -24 to 24
Outputs:
- regrouped: bfloat16 [2048, 8192], P(('dp', 'head'))
- hessian: float32 [8192, 8192], P('dp', 'head')
The draws below stay inside these ranges and needn't reach their ends.
All inputs are finite; a program needn't handle non-finite values.
Results may differ from the reference program's by a relative error of at most 0.0044.
Values may be sent and summed in bfloat16 or wider, within the bound.
A program may use at most 128 MiB of HBM per device.

```python
import math
import jax
import jax.numpy as jnp
from jax import lax

HEADS = 64
HEAD_SIZE = 128
D = 8192
LEN = 1024
TOKENS = 2048


def paired_fields(base_key):
    query_key, other_key = jax.random.split(base_key, 2)
    query_vals = jnp.clip(2.5 * jax.random.normal(query_key, (TOKENS, D), jnp.float32), -14.0, 14.0)
    key_vals = jnp.clip(2.5 * jax.random.normal(other_key, (TOKENS, D), jnp.float32), -14.0, 14.0)
    return (query_vals, key_vals)


def draw_queries(key, part):
    return paired_fields(jax.random.fold_in(key, 11))[0].astype(jnp.bfloat16)


def draw_keys(key, part):
    return paired_fields(jax.random.fold_in(key, 11))[1].astype(jnp.bfloat16)


def spiked(values, rng, source, target, shards_of, factor):
    def block_of(position):
        return (jnp.arange(values.shape[position]) // (values.shape[position] // shards_of)).reshape((-1,) + (1,) * (values.ndim - 1 - position))

    near = jax.random.permutation(rng, shards_of)[block_of(target)]
    other_side = (block_of(target) + shards_of // 2) % shards_of
    return jnp.where((block_of(source) == near) | (block_of(source) == other_side), factor * values, values)


def shard_levels(key, dims, pieces, smallest, high):
    def one(position, blocks):
        steps = jax.random.uniform(jax.random.fold_in(jax.random.fold_in(key, 6), position), (blocks,), jnp.float32, smallest / len(pieces), high / len(pieces))
        return jnp.repeat(jnp.exp(steps), dims[position] // blocks).reshape((-1,) + (1,) * (len(dims) - position - 1))

    factor_of = one(*pieces[0])
    for cut in pieces[1:]:
        factor_of = factor_of * one(*cut)
    return factor_of


def heavy_noise(stream_key, shape, deviation, bound, cuts, heavy, held_as=jnp.bfloat16):
    drawn = deviation * jax.random.normal(stream_key, shape, jnp.float32)
    if cuts:
        drawn = drawn * shard_levels(stream_key, shape, cuts, -0.22, 0.18)
    return jnp.clip(spiked(drawn, jax.random.fold_in(stream_key, 3), *heavy), -bound, bound).astype(held_as)


def setup_inputs(seed: int = 0) -> dict:
    key_of = jax.random.split(jax.random.key(seed), 4)
    return {
        "queries": draw_queries(jax.random.fold_in(key_of[3], 71), 0),
        "keys": draw_keys(jax.random.fold_in(key_of[3], 71), 0),
        "values": heavy_noise(key_of[2], (TOKENS, D), 4.0, 24.0, ((0, 2), (1, 16)), (0, 1, 16, 2.0)),
    }


def head_attention(operands):
    head_query_rows, head_key_rows, head_value_rows = operands
    logit_matrix = jnp.einsum('ixy,ijy->ixj', head_query_rows.astype(jnp.float32), head_key_rows.astype(jnp.float32)) * (1.0 / math.sqrt(HEAD_SIZE))
    causal = lax.broadcasted_iota(jnp.int32, (LEN, LEN), 0) >= lax.broadcasted_iota(jnp.int32, (LEN, LEN), 1)
    logit_matrix = jnp.where(causal[None], logit_matrix, -1e+30)
    peak = lax.optimization_barrier(jnp.max(logit_matrix, axis=-1, keepdims=True))
    raised = jnp.exp(logit_matrix - peak)
    attention_weight = (raised / lax.optimization_barrier(jnp.sum(raised, axis=-1, keepdims=True))).astype(jnp.bfloat16)
    attended_values = jnp.einsum('fjh,fhu->fju', attention_weight.astype(jnp.float32), head_value_rows.astype(jnp.float32))
    return attended_values.astype(jnp.bfloat16)

def reference(queries, keys, values):
    groups = TOKENS // LEN

    def split_heads(array):
        return jnp.transpose(array.reshape(groups, LEN, HEADS, HEAD_SIZE), (2, 0, 1, 3))
    outputs = lax.map(head_attention, (split_heads(queries), split_heads(keys), split_heads(values)))
    regrouped = jnp.transpose(outputs, (1, 2, 0, 3)).reshape(TOKENS, D)
    widened = regrouped.astype(jnp.float32)
    hessian = jnp.dot(widened.T, widened, precision=lax.Precision.HIGHEST) * (2.0 / TOKENS)
    return (regrouped, hessian)
```

```python
import math

import jax
import jax.numpy as jnp
from jax import lax
from jax.sharding import PartitionSpec as P

HEAD_SIZE = 128


def attend(queries, keys, values):
    rows_local = queries.shape[0]
    heads_local = queries.shape[1] // HEAD_SIZE
    query_heads = queries.reshape(rows_local, heads_local, HEAD_SIZE)
    key_heads = keys.reshape(rows_local, heads_local, HEAD_SIZE)
    value_heads = values.reshape(rows_local, heads_local, HEAD_SIZE)
    logit_matrix = jnp.einsum(
        "qhd,khd->hqk", query_heads, key_heads, preferred_element_type=jnp.float32
    ) * (1.0 / math.sqrt(HEAD_SIZE))
    causal = lax.broadcasted_iota(jnp.int32, (rows_local, rows_local), 0) >= lax.broadcasted_iota(
        jnp.int32, (rows_local, rows_local), 1
    )
    logit_matrix = jnp.where(causal[None], logit_matrix, -1e30)
    peak = jnp.max(logit_matrix, axis=-1, keepdims=True)
    raised = jnp.exp(logit_matrix - peak)
    attention_weight = (raised / jnp.sum(raised, axis=-1, keepdims=True)).astype(jnp.bfloat16)
    attended_values = jnp.einsum(
        "hqk,khd->qhd", attention_weight, value_heads, preferred_element_type=jnp.float32
    )
    return attended_values.astype(jnp.bfloat16).reshape(rows_local, heads_local * HEAD_SIZE)


def body(queries, keys, values):
    outputs = attend(queries, keys, values)
    rows, cols = outputs.shape
    groups = lax.axis_size("dp")
    heads = lax.axis_size("head")
    me = lax.axis_index("dp")
    position = lax.axis_index("head")
    scale = 2.0 / (rows * groups)
    chunks = 2 if cols % 256 == 0 else 1
    width = cols // chunks
    rows_out = rows // heads
    pieces, sums = [], []
    for c in range(chunks):
        part = outputs[:, c * width : (c + 1) * width]
        gathered = lax.all_gather(part, "head", axis=0, tiled=False)
        mine = lax.dynamic_slice_in_dim(gathered, position * rows_out, rows_out, axis=1)
        pieces.append(jnp.swapaxes(mine, 0, 1))

        def term(owner):
            block = lax.dynamic_slice_in_dim(
                gathered, owner * (heads // groups), heads // groups, axis=0
            )
            return jnp.einsum("htf,tc->hfc", block, outputs, preferred_element_type=jnp.float32)

        arrived = []
        for shift in range(1, groups):
            sent = term(lax.rem(me + shift, groups)).astype(jnp.bfloat16)
            pairs = [(g, (g + shift) % groups) for g in range(groups)]
            arrived.append(lax.ppermute(sent, "dp", pairs))
        total = term(me)
        for other in arrived:
            total = total + other.astype(jnp.float32)
        sums.append(total * scale)
    regrouped = jnp.concatenate(pieces, axis=2).reshape(rows_out, heads * cols)
    hessian = jnp.concatenate(sums, axis=1).reshape(heads * cols // groups, cols)
    return (regrouped, hessian)


def solution(mesh):
    in_specs = (P("dp", "head"), P("dp", "head"), P("dp", "head"))
    out_specs = (P(("dp", "head"), None), P("dp", "head"))
    return jax.shard_map(body, mesh=mesh, in_specs=in_specs, out_specs=out_specs, check_vma=False)
```

```python
import functools
import math

import jax
import jax.numpy as jnp
from jax import lax
from jax.experimental import pallas as pl
from jax.experimental.pallas import tpu as pltpu
from jax.sharding import PartitionSpec as P

HEAD_SIZE = 128
MESH = pl.DeviceIdType.MESH


def attend(queries, keys, values):
    rows_local = queries.shape[0]
    heads_local = queries.shape[1] // HEAD_SIZE
    query_heads = queries.reshape(rows_local, heads_local, HEAD_SIZE)
    key_heads = keys.reshape(rows_local, heads_local, HEAD_SIZE)
    value_heads = values.reshape(rows_local, heads_local, HEAD_SIZE)
    logit_matrix = jnp.einsum(
        "qhd,khd->hqk", query_heads, key_heads, preferred_element_type=jnp.float32
    ) * (1.0 / math.sqrt(HEAD_SIZE))
    causal = lax.broadcasted_iota(jnp.int32, (rows_local, rows_local), 0) >= lax.broadcasted_iota(
        jnp.int32, (rows_local, rows_local), 1
    )
    logit_matrix = jnp.where(causal[None], logit_matrix, -1e30)
    peak = jnp.max(logit_matrix, axis=-1, keepdims=True)
    raised = jnp.exp(logit_matrix - peak)
    attention_weight = (raised / jnp.sum(raised, axis=-1, keepdims=True)).astype(jnp.bfloat16)
    attended_values = jnp.einsum(
        "hqk,khd->qhd", attention_weight, value_heads, preferred_element_type=jnp.float32
    )
    return attended_values.astype(jnp.bfloat16).reshape(rows_local, heads_local * HEAD_SIZE)


def exchange_kernel(
    groups, heads, scale,
    own_ref, regrouped_ref, hessian_ref,
    gathered, total, leaving, arrived,
    ring_send, ring_recv, pair_send, pair_recv, sum_send, sum_recv,
    load_sem, rows_sem, out_sem,
):
    rows, cols = own_ref.shape
    half = rows // 2
    chips = heads // 2
    depth = chips // 2
    per_group = heads // groups
    rows_out = rows // heads
    tile = min(cols, 256)
    me = lax.axis_index("dp")
    here = lax.axis_index("head")
    core = lax.rem(here, 2)
    chip = lax.div(here, 2)
    layers = chips // 2
    side = lax.rem(chip, 2)
    level = lax.div(chip, 2)
    place = level + side * (2 * layers - 1 - 2 * level)

    def head_at(position, which):
        spot = lax.rem(position + 2 * chips, chips)
        far = lax.div(spot, layers)
        height = spot + far * (2 * layers - 1 - 2 * spot)
        return (height * 2 + far) * 2 + which

    right = head_at(place + 1, core)
    left = head_at(place - 1, core)
    partner = here + 1 - 2 * core

    load = pltpu.make_async_copy(own_ref, gathered.at[here], load_sem)
    load.start()
    barrier = pltpu.get_barrier_semaphore()
    for other in (right, left, partner):
        pl.semaphore_signal(barrier, inc=1, device_id=(me, other), device_id_type=MESH)
    for shift in range(1, groups):
        pl.semaphore_signal(
            barrier, inc=1, device_id=(lax.rem(me + shift, groups), here), device_id_type=MESH
        )
    pl.semaphore_wait(barrier, 3 + groups - 1)
    load.wait()

    def block(head, part):
        return gathered.at[head, pl.ds(part * half, half)]

    def ring(direction, part, step):
        source = head_at(place + step * (2 * direction - 1), core)
        ref = block(source, part)
        return pltpu.make_async_remote_copy(
            src_ref=ref, dst_ref=ref,
            send_sem=ring_send.at[direction, part, step],
            recv_sem=ring_recv.at[direction, part, step],
            device_id=(me, right if direction == 0 else left), device_id_type=MESH,
        )

    def ring_arrival(direction, part, step):
        source = head_at(place + step * (2 * direction - 1), core)
        ref = block(source, part)
        return pltpu.make_async_remote_copy(
            src_ref=ref, dst_ref=ref,
            send_sem=ring_send.at[direction, part, step - 1],
            recv_sem=ring_recv.at[direction, part, step - 1],
            device_id=(me, right if direction == 0 else left), device_id_type=MESH,
        )

    def pair(direction, part, step, which):
        ref = block(head_at(place + step * (2 * direction - 1), which), part)
        return pltpu.make_async_remote_copy(
            src_ref=ref, dst_ref=ref,
            send_sem=pair_send.at[direction, part, step],
            recv_sem=pair_recv.at[direction, part, step],
            device_id=(me, partner), device_id_type=MESH,
        )

    def sum_copy(shift, local):
        return pltpu.make_async_remote_copy(
            src_ref=leaving.at[shift - 1, local], dst_ref=arrived.at[shift - 1, local],
            send_sem=sum_send.at[shift - 1, local], recv_sem=sum_recv.at[shift - 1, local],
            device_id=(lax.rem(me + shift, groups), here), device_id_type=MESH,
        )

    def rows_copy(head):
        return pltpu.make_async_copy(
            gathered.at[head, pl.ds(pl.multiple_of(here * rows_out, rows_out), rows_out)],
            regrouped_ref.at[:, pl.ds(pl.multiple_of(head * cols, cols), cols)],
            rows_sem.at[head],
        )

    def out_copy(local):
        return pltpu.make_async_copy(
            total.at[local],
            hessian_ref.at[pl.ds(pl.multiple_of(local * cols, cols), cols)],
            out_sem.at[local],
        )

    def gram(head):
        rows_copy(head).start()
        owner = lax.div(head, per_group)
        local = lax.rem(head, per_group)
        shift = lax.rem(owner - me + groups, groups)

        def one(t, carry):
            where = pl.ds(pl.multiple_of(t * tile, tile), tile)
            term = lax.dot_general(
                gathered[head, :, where], gathered[here],
                (((0,), (0,)), ((), ())), preferred_element_type=jnp.float32,
            )

            @pl.when(shift == 0)
            def _():
                total[local, where] = term

            @pl.when(shift != 0)
            def _():
                leaving[shift - 1, local, where] = term.astype(jnp.bfloat16)

            return carry

        lax.fori_loop(0, cols // tile, one, 0)

        @pl.when(shift != 0)
        def _():
            sum_copy(shift, local).start()

    reach = {(0, 0): depth, (1, 0): depth - 1, (0, 1): depth - 1, (1, 1): depth}
    for part in range(2):
        for direction in range(2):
            ring(direction, part, 0).start()
    for part in range(2):
        pair(0, part, 0, core).start()
    gram(here)

    def receive(part, step):
        for direction in range(2):
            ring_arrival(direction, part, step).wait_recv()
            if reach[direction, part] == depth:
                ring(direction, part, step).start()
            else:
                @pl.when(step < depth - 1)
                def _():
                    ring(direction, part, step).start()
            pair(direction, part, step, core).start()

    def pair_arrivals(step):
        for part in range(2):
            for direction in range(2):
                pair(direction, part, step, 1 - core).wait_recv()

    def advance(step, carry):
        receive(0, step)

        @pl.when(step == 1)
        def _():
            for part in range(2):
                pair(0, part, 0, 1 - core).wait_recv()
            gram(partner)

        @pl.when(step > 1)
        def _():
            pair_arrivals(step - 1)
            gram(head_at(place - step + 1, 1 - core))
            gram(head_at(place + step - 1, 1 - core))

        receive(1, step)
        gram(head_at(place - step, core))
        gram(head_at(place + step, core))
        return carry

    lax.fori_loop(1, depth, advance, 0)
    for direction, part in ((0, 0), (1, 1)):
        ring_arrival(direction, part, depth).wait_recv()
        pair(direction, part, depth, core).start()
    if depth > 1:
        pair_arrivals(depth - 1)
        gram(head_at(place - depth + 1, 1 - core))
        gram(head_at(place + depth - 1, 1 - core))
    gram(head_at(place - depth, core))
    for direction, part in ((0, 0), (1, 1)):
        pair(direction, part, depth, 1 - core).wait_recv()
    gram(head_at(place - depth, 1 - core))

    def finish(order, carry):
        away = lax.div(order, 4)
        kind = lax.rem(order, 4)
        head = head_at(
            place + (away + 1) * (2 * lax.rem(kind, 2) - 1), lax.rem(core + lax.div(kind, 2), 2)
        )
        collect(head)
        return carry

    def collect(head):
        owner = lax.div(head, per_group)
        local = lax.rem(head, per_group)

        @pl.when(owner == me)
        def _():
            for shift in range(1, groups):
                sum_copy(shift, local).wait_recv()
            value = total[local]
            for shift in range(1, groups):
                value = value + arrived[shift - 1, local].astype(jnp.float32)
            total[local] = value * scale
            out_copy(local).start()

    collect(here)
    collect(partner)
    lax.fori_loop(0, 4 * (depth - 1), finish, 0)
    collect(head_at(place - depth, core))
    collect(head_at(place - depth, 1 - core))

    def drain(head, carry):
        rows_copy(head).wait()
        owner = lax.div(head, per_group)
        local = lax.rem(head, per_group)
        shift = lax.rem(owner - me + groups, groups)

        @pl.when(shift != 0)
        def _():
            sum_copy(shift, local).wait_send()

        @pl.when(shift == 0)
        def _():
            out_copy(local).wait()

        return carry

    lax.fori_loop(0, heads, drain, 0)

    def drain_sends(step, carry):
        for (direction, part), distance in reach.items():
            @pl.when(step < distance)
            def _():
                ring(direction, part, step).wait_send()

            @pl.when((step > 0) & (step <= distance))
            def _():
                pair(direction, part, step, core).wait_send()
        return carry

    lax.fori_loop(0, depth + 1, drain_sends, 0)
    for part in range(2):
        pair(0, part, 0, core).wait_send()


def exchange(outputs, groups, heads):
    rows, cols = outputs.shape
    per_group = heads // groups
    depth = heads // 4
    dma = pltpu.SemaphoreType.DMA
    return pl.pallas_call(
        functools.partial(exchange_kernel, groups, heads, 2.0 / (rows * groups)),
        out_shape=(
            jax.ShapeDtypeStruct((rows // heads, heads * cols), jnp.bfloat16),
            jax.ShapeDtypeStruct((per_group * cols, cols), jnp.float32),
        ),
        in_specs=[pl.BlockSpec(memory_space=pl.ANY)],
        out_specs=(pl.BlockSpec(memory_space=pl.ANY), pl.BlockSpec(memory_space=pl.ANY)),
        scratch_shapes=[
            pltpu.VMEM((heads, rows, cols), jnp.bfloat16),
            pltpu.VMEM((per_group, cols, cols), jnp.float32),
            pltpu.VMEM((groups - 1, per_group, cols, cols), jnp.bfloat16),
            pltpu.VMEM((groups - 1, per_group, cols, cols), jnp.bfloat16),
            dma((2, 2, depth)),
            dma((2, 2, depth)),
            dma((2, 2, depth + 1)),
            dma((2, 2, depth + 1)),
            dma((groups - 1, per_group)),
            dma((groups - 1, per_group)),
            dma,
            dma((heads,)),
            dma((per_group,)),
        ],
        compiler_params=pltpu.CompilerParams(
            collective_id=0, has_side_effects=True, vmem_limit_bytes=56 * 1024 * 1024
        ),
    )(outputs)


def body(queries, keys, values):
    outputs = attend(queries, keys, values)
    return exchange(outputs, lax.axis_size("dp"), lax.axis_size("head"))


def solution(mesh):
    in_specs = (P("dp", "head"), P("dp", "head"), P("dp", "head"))
    out_specs = (P(("dp", "head"), None), P("dp", "head"))
    return jax.shard_map(body, mesh=mesh, in_specs=in_specs, out_specs=out_specs, check_vma=False)
```

```python
import functools
import math

import jax
import jax.numpy as jnp
from jax import lax
from jax.experimental import pallas as pl
from jax.experimental.pallas import tpu as pltpu
from jax.sharding import PartitionSpec as P

HEAD_SIZE = 128
MESH = pl.DeviceIdType.MESH


def exchange_kernel(
    groups, heads, scale,
    query_ref, key_ref, value_ref, regrouped_ref, total,
    gathered, leaving, arrived,
    ring_send, ring_recv, pair_send, pair_recv, sum_send, sum_recv,
    rows_sem,
):
    rows, cols = query_ref.shape
    half = rows // 2
    quarter = rows // 4
    chips = heads // 2
    depth = chips // 2
    per_group = heads // groups
    rows_out = rows // heads
    tile = min(cols, 256)
    me = lax.axis_index("dp")
    here = lax.axis_index("head")
    core = lax.rem(here, 2)
    chip = lax.div(here, 2)
    layers = chips // 2
    side = lax.rem(chip, 2)
    level = lax.div(chip, 2)
    place = level + side * (2 * layers - 1 - 2 * level)

    def head_at(position, which):
        spot = lax.rem(position + 2 * chips, chips)
        far = lax.div(spot, layers)
        height = spot + far * (2 * layers - 1 - 2 * spot)
        return (height * 2 + far) * 2 + which

    right = head_at(place + 1, core)
    left = head_at(place - 1, core)
    partner = here + 1 - 2 * core

    barrier = pltpu.get_barrier_semaphore()
    for other in (right, left, partner):
        pl.semaphore_signal(barrier, inc=1, device_id=(me, other), device_id_type=MESH)
    for shift in range(1, groups):
        pl.semaphore_signal(
            barrier, inc=1, device_id=(lax.rem(me + shift, groups), here), device_id_type=MESH
        )

    def attend(part):
        def head_of(index, carry):
            lanes = pl.ds(pl.multiple_of(index * HEAD_SIZE, HEAD_SIZE), HEAD_SIZE)
            for strip in range(2 * part, 2 * part + 2):
                seen = (strip + 1) * quarter
                here_rows = pl.ds(strip * quarter, quarter)
                logits = lax.dot_general(
                    query_ref[here_rows, lanes], key_ref[pl.ds(0, seen), lanes],
                    (((1,), (1,)), ((), ())), preferred_element_type=jnp.float32,
                ) * (1.0 / math.sqrt(HEAD_SIZE))
                row = lax.broadcasted_iota(jnp.int32, logits.shape, 0) + strip * quarter
                column = lax.broadcasted_iota(jnp.int32, logits.shape, 1)
                logits = jnp.where(row >= column, logits, -1e30)
                raised = jnp.exp(logits - jnp.max(logits, axis=-1, keepdims=True))
                weight = raised * (1.0 / jnp.sum(raised, axis=-1, keepdims=True))
                gathered[here, here_rows, lanes] = jnp.dot(
                    weight.astype(jnp.bfloat16), value_ref[pl.ds(0, seen), lanes],
                    preferred_element_type=jnp.float32,
                ).astype(jnp.bfloat16)
            return carry

        lax.fori_loop(0, cols // HEAD_SIZE, head_of, 0)

    def block(head, part):
        return gathered.at[head, pl.ds(part * half, half)]

    def ring(direction, part, step):
        source = head_at(place + step * (2 * direction - 1), core)
        ref = block(source, part)
        return pltpu.make_async_remote_copy(
            src_ref=ref, dst_ref=ref,
            send_sem=ring_send.at[direction, part, step],
            recv_sem=ring_recv.at[direction, part, step],
            device_id=(me, right if direction == 0 else left), device_id_type=MESH,
        )

    def ring_arrival(direction, part, step):
        source = head_at(place + step * (2 * direction - 1), core)
        ref = block(source, part)
        return pltpu.make_async_remote_copy(
            src_ref=ref, dst_ref=ref,
            send_sem=ring_send.at[direction, part, step - 1],
            recv_sem=ring_recv.at[direction, part, step - 1],
            device_id=(me, right if direction == 0 else left), device_id_type=MESH,
        )

    def pair(direction, part, step, which):
        ref = block(head_at(place + step * (2 * direction - 1), which), part)
        return pltpu.make_async_remote_copy(
            src_ref=ref, dst_ref=ref,
            send_sem=pair_send.at[direction, part, step],
            recv_sem=pair_recv.at[direction, part, step],
            device_id=(me, partner), device_id_type=MESH,
        )

    def sum_copy(shift, local):
        return pltpu.make_async_remote_copy(
            src_ref=leaving.at[shift - 1, local], dst_ref=arrived.at[shift - 1, local],
            send_sem=sum_send.at[shift - 1, local], recv_sem=sum_recv.at[shift - 1, local],
            device_id=(lax.rem(me + shift, groups), here), device_id_type=MESH,
        )

    def rows_copy(head):
        return pltpu.make_async_copy(
            gathered.at[head, pl.ds(pl.multiple_of(here * rows_out, rows_out), rows_out)],
            regrouped_ref.at[:, pl.ds(pl.multiple_of(head * cols, cols), cols)],
            rows_sem.at[head],
        )

    def gram(head):
        rows_copy(head).start()
        owner = lax.div(head, per_group)
        local = lax.rem(head, per_group)
        shift = lax.rem(owner - me + groups, groups)

        def one(t, carry):
            where = pl.ds(pl.multiple_of(t * tile, tile), tile)
            term = lax.dot_general(
                gathered[head, :, where], gathered[here],
                (((0,), (0,)), ((), ())), preferred_element_type=jnp.float32,
            )

            @pl.when(shift == 0)
            def _():
                total[local, where] = term

            @pl.when(shift != 0)
            def _():
                leaving[shift - 1, local, where] = term.astype(jnp.bfloat16)

            return carry

        lax.fori_loop(0, cols // tile, one, 0)

        @pl.when(shift != 0)
        def _():
            sum_copy(shift, local).start()

    reach = {(0, 0): depth, (1, 0): depth - 1, (0, 1): depth - 1, (1, 1): depth}
    for part in range(2):
        attend(part)
        if part == 0:
            pl.semaphore_wait(barrier, 3 + groups - 1)
        for direction in range(2):
            ring(direction, part, 0).start()
        pair(0, part, 0, core).start()
    gram(here)

    def receive(part, step):
        for direction in range(2):
            ring_arrival(direction, part, step).wait_recv()
            if reach[direction, part] == depth:
                ring(direction, part, step).start()
            else:
                @pl.when(step < depth - 1)
                def _():
                    ring(direction, part, step).start()
            pair(direction, part, step, core).start()

    def pair_arrivals(step):
        for part in range(2):
            for direction in range(2):
                pair(direction, part, step, 1 - core).wait_recv()

    def advance(step, carry):
        receive(0, step)

        @pl.when(step == 1)
        def _():
            for part in range(2):
                pair(0, part, 0, 1 - core).wait_recv()
            gram(partner)

        @pl.when(step > 1)
        def _():
            pair_arrivals(step - 1)
            gram(head_at(place - step + 1, 1 - core))
            gram(head_at(place + step - 1, 1 - core))

        receive(1, step)
        gram(head_at(place - step, core))
        gram(head_at(place + step, core))
        return carry

    lax.fori_loop(1, depth, advance, 0)
    for direction, part in ((0, 0), (1, 1)):
        ring_arrival(direction, part, depth).wait_recv()
        pair(direction, part, depth, core).start()
    if depth > 1:
        pair_arrivals(depth - 1)
        gram(head_at(place - depth + 1, 1 - core))
        gram(head_at(place + depth - 1, 1 - core))
    gram(head_at(place - depth, core))
    for direction, part in ((0, 0), (1, 1)):
        pair(direction, part, depth, 1 - core).wait_recv()
    gram(head_at(place - depth, 1 - core))

    def finish(order, carry):
        away = lax.div(order, 4)
        kind = lax.rem(order, 4)
        head = head_at(
            place + (away + 1) * (2 * lax.rem(kind, 2) - 1), lax.rem(core + lax.div(kind, 2), 2)
        )
        collect(head)
        return carry

    def collect(head):
        owner = lax.div(head, per_group)
        local = lax.rem(head, per_group)

        @pl.when(owner == me)
        def _():
            for shift in range(1, groups):
                sum_copy(shift, local).wait_recv()
            value = total[local]
            for shift in range(1, groups):
                value = value + arrived[shift - 1, local].astype(jnp.float32)
            total[local] = value * scale

    collect(here)
    collect(partner)
    lax.fori_loop(0, 4 * (depth - 1), finish, 0)
    collect(head_at(place - depth, core))
    collect(head_at(place - depth, 1 - core))

    def drain(head, carry):
        rows_copy(head).wait()
        owner = lax.div(head, per_group)
        local = lax.rem(head, per_group)
        shift = lax.rem(owner - me + groups, groups)

        @pl.when(shift != 0)
        def _():
            sum_copy(shift, local).wait_send()

        return carry

    lax.fori_loop(0, heads, drain, 0)

    def drain_sends(step, carry):
        for (direction, part), distance in reach.items():
            @pl.when(step < distance)
            def _():
                ring(direction, part, step).wait_send()

            @pl.when((step > 0) & (step <= distance))
            def _():
                pair(direction, part, step, core).wait_send()
        return carry

    lax.fori_loop(0, depth + 1, drain_sends, 0)
    for part in range(2):
        pair(0, part, 0, core).wait_send()


def exchange(queries, keys, values, groups, heads):
    rows, cols = queries.shape
    per_group = heads // groups
    depth = heads // 4
    dma = pltpu.SemaphoreType.DMA
    vmem = pl.BlockSpec(memory_space=pltpu.VMEM)
    return pl.pallas_call(
        functools.partial(exchange_kernel, groups, heads, 2.0 / (rows * groups)),
        out_shape=(
            pltpu.VMEM((rows // heads, heads * cols), jnp.bfloat16),
            pltpu.VMEM((per_group, cols, cols), jnp.float32),
        ),
        in_specs=[vmem, vmem, vmem],
        out_specs=(vmem, vmem),
        scratch_shapes=[
            pltpu.VMEM((heads, rows, cols), jnp.bfloat16),
            pltpu.VMEM((groups - 1, per_group, cols, cols), jnp.bfloat16),
            pltpu.VMEM((groups - 1, per_group, cols, cols), jnp.bfloat16),
            dma((2, 2, depth)),
            dma((2, 2, depth)),
            dma((2, 2, depth + 1)),
            dma((2, 2, depth + 1)),
            dma((groups - 1, per_group)),
            dma((groups - 1, per_group)),
            dma((heads,)),
        ],
        compiler_params=pltpu.CompilerParams(
            collective_id=0, has_side_effects=True, vmem_limit_bytes=40 * 1024 * 1024
        ),
    )(queries, keys, values)


def body(queries, keys, values):
    cols = queries.shape[1]
    regrouped, total = exchange(
        queries, keys, values, lax.axis_size("dp"), lax.axis_size("head")
    )
    return (regrouped, total.reshape(-1, cols))


def solution(mesh):
    in_specs = (P("dp", "head"), P("dp", "head"), P("dp", "head"))
    out_specs = (P(("dp", "head"), None), P("dp", "head"))
    return jax.shard_map(body, mesh=mesh, in_specs=in_specs, out_specs=out_specs, check_vma=False)
```

```python
import functools
import math

import jax
import jax.numpy as jnp
from jax import lax
from jax.experimental import pallas as pl
from jax.experimental.pallas import tpu as pltpu
from jax.sharding import PartitionSpec as P

HEAD_SIZE = 128
MESH = pl.DeviceIdType.MESH


def exchange_kernel(
    groups, heads, scale,
    query_hbm, key_hbm, value_hbm, regrouped_ref, total,
    query_ref, key_ref, value_ref, gathered, leaving, arrived, lent,
    ring_send, ring_recv, pair_send, pair_recv, sum_send, sum_recv,
    rows_sem, load_sem, lent_send,
):
    rows, cols = query_ref.shape
    half = rows // 2
    quarter = rows // 4
    chips = heads // 2
    depth = chips // 2
    per_group = heads // groups
    rows_out = rows // heads
    tile = min(cols, 256)
    me = lax.axis_index("dp")
    here = lax.axis_index("head")
    core = lax.rem(here, 2)
    chip = lax.div(here, 2)
    layers = chips // 2
    side = lax.rem(chip, 2)
    level = lax.div(chip, 2)
    place = level + side * (2 * layers - 1 - 2 * level)

    def head_at(position, which):
        spot = lax.rem(position + 2 * chips, chips)
        far = lax.div(spot, layers)
        height = spot + far * (2 * layers - 1 - 2 * spot)
        return (height * 2 + far) * 2 + which

    right = head_at(place + 1, core)
    left = head_at(place - 1, core)
    partner = here + 1 - 2 * core

    loads = [
        pltpu.make_async_copy(source, target, load_sem.at[n])
        for n, (source, target) in enumerate(
            ((query_hbm, query_ref), (key_hbm, key_ref), (value_hbm, value_ref))
        )
    ]
    for load in loads:
        load.start()
    lending = groups == 2
    lends = level == (layers - 1) * me
    borrows = level == (layers - 1) * (1 - me)
    mirror = ((layers - 1 - level) * 2 + side) * 2 + core

    barrier = pltpu.get_barrier_semaphore()
    if lending:
        pl.semaphore_signal(barrier, inc=1, device_id=(1 - me, mirror), device_id_type=MESH)
    for other in (right, left, partner):
        pl.semaphore_signal(barrier, inc=1, device_id=(me, other), device_id_type=MESH)
    for shift in range(1, groups):
        pl.semaphore_signal(
            barrier, inc=1, device_id=(lax.rem(me + shift, groups), here), device_id_type=MESH
        )

    def attend(part):
        def head_of(index, carry):
            lanes = pl.ds(pl.multiple_of(index * HEAD_SIZE, HEAD_SIZE), HEAD_SIZE)
            for strip in range(2 * part, 2 * part + 2):
                seen = (strip + 1) * quarter
                here_rows = pl.ds(strip * quarter, quarter)
                logits = lax.dot_general(
                    query_ref[here_rows, lanes], key_ref[pl.ds(0, seen), lanes],
                    (((1,), (1,)), ((), ())), preferred_element_type=jnp.float32,
                ) * (1.0 / math.sqrt(HEAD_SIZE))
                row = lax.broadcasted_iota(jnp.int32, logits.shape, 0) + strip * quarter
                column = lax.broadcasted_iota(jnp.int32, logits.shape, 1)
                logits = jnp.where(row >= column, logits, -1e30)
                raised = jnp.exp(logits - jnp.max(logits, axis=-1, keepdims=True))
                weight = raised * (1.0 / jnp.sum(raised, axis=-1, keepdims=True))
                gathered[here, here_rows, lanes] = jnp.dot(
                    weight.astype(jnp.bfloat16), value_ref[pl.ds(0, seen), lanes],
                    preferred_element_type=jnp.float32,
                ).astype(jnp.bfloat16)
            return carry

        lax.fori_loop(0, cols // HEAD_SIZE, head_of, 0)

    def block(head, part):
        return gathered.at[head, pl.ds(part * half, half)]

    def ring(direction, part, step):
        source = head_at(place + step * (2 * direction - 1), core)
        ref = block(source, part)
        return pltpu.make_async_remote_copy(
            src_ref=ref, dst_ref=ref,
            send_sem=ring_send.at[direction, part, step],
            recv_sem=ring_recv.at[direction, part, step],
            device_id=(me, right if direction == 0 else left), device_id_type=MESH,
        )

    def ring_arrival(direction, part, step):
        source = head_at(place + step * (2 * direction - 1), core)
        ref = block(source, part)
        return pltpu.make_async_remote_copy(
            src_ref=ref, dst_ref=ref,
            send_sem=ring_send.at[direction, part, step - 1],
            recv_sem=ring_recv.at[direction, part, step - 1],
            device_id=(me, right if direction == 0 else left), device_id_type=MESH,
        )

    def pair(direction, part, step, which):
        ref = block(head_at(place + step * (2 * direction - 1), which), part)
        return pltpu.make_async_remote_copy(
            src_ref=ref, dst_ref=ref,
            send_sem=pair_send.at[direction, part, step],
            recv_sem=pair_recv.at[direction, part, step],
            device_id=(me, partner), device_id_type=MESH,
        )

    def sum_copy(shift, local):
        return pltpu.make_async_remote_copy(
            src_ref=leaving.at[shift - 1, local], dst_ref=arrived.at[shift - 1, local],
            send_sem=sum_send.at[shift - 1, local], recv_sem=sum_recv.at[shift - 1, local],
            device_id=(lax.rem(me + shift, groups), here), device_id_type=MESH,
        )

    def rows_copy(head):
        return pltpu.make_async_copy(
            gathered.at[head, pl.ds(pl.multiple_of(here * rows_out, rows_out), rows_out)],
            regrouped_ref.at[:, pl.ds(pl.multiple_of(head * cols, cols), cols)],
            rows_sem.at[head],
        )

    def gram(head):
        rows_copy(head).start()
        owner = lax.div(head, per_group)
        local = lax.rem(head, per_group)
        shift = lax.rem(owner - me + groups, groups)

        def one(t, carry):
            where = pl.ds(pl.multiple_of(t * tile, tile), tile)
            term = lax.dot_general(
                gathered[head, :, where], gathered[here],
                (((0,), (0,)), ((), ())), preferred_element_type=jnp.float32,
            )

            @pl.when(shift == 0)
            def _():
                total[local, where] = term

            @pl.when(shift != 0)
            def _():
                leaving[shift - 1, local, where] = term.astype(jnp.bfloat16)

            return carry

        lax.fori_loop(0, cols // tile, one, 0)

        @pl.when(shift != 0)
        def _():
            sum_copy(shift, local).start()

    def lent_copy(which):
        local = lax.rem((level * 2 + 1 - side) * 2 + which, per_group)
        return pltpu.make_async_remote_copy(
            src_ref=lent.at[which], dst_ref=arrived.at[0, local],
            send_sem=lent_send.at[which], recv_sem=sum_recv.at[0, local],
            device_id=(1 - me, mirror), device_id_type=MESH,
        )

    def gram_for_mirror(which):
        head = (level * 2 + 1 - side) * 2 + which

        def one(t, carry):
            where = pl.ds(pl.multiple_of(t * tile, tile), tile)
            lent[which, where] = lax.dot_general(
                gathered[head, :, where], gathered[mirror],
                (((0,), (0,)), ((), ())), preferred_element_type=jnp.float32,
            ).astype(jnp.bfloat16)
            return carry

        lax.fori_loop(0, cols // tile, one, 0)
        lent_copy(which).start()

    def gram_far(head):
        if not lending:
            gram(head)
            return

        @pl.when(lends)
        def _():
            rows_copy(head).start()

        @pl.when(jnp.logical_not(lends))
        def _():
            gram(head)

    reach = {(0, 0): depth, (1, 0): depth - 1, (0, 1): depth - 1, (1, 1): depth}
    for load in loads:
        load.wait()
    for part in range(2):
        attend(part)
        if part == 0:
            pl.semaphore_wait(barrier, 3 + groups - 1 + int(lending))
        for direction in range(2):
            ring(direction, part, 0).start()
        pair(0, part, 0, core).start()
    gram(here)

    def receive(part, step):
        for direction in range(2):
            ring_arrival(direction, part, step).wait_recv()
            if reach[direction, part] == depth:
                ring(direction, part, step).start()
            else:
                @pl.when(step < depth - 1)
                def _():
                    ring(direction, part, step).start()
            pair(direction, part, step, core).start()

    def pair_arrivals(step):
        for part in range(2):
            for direction in range(2):
                pair(direction, part, step, 1 - core).wait_recv()

    def advance(step, carry):
        receive(0, step)

        @pl.when(step == 1)
        def _():
            for part in range(2):
                pair(0, part, 0, 1 - core).wait_recv()
            gram(partner)

        @pl.when(step > 1)
        def _():
            pair_arrivals(step - 1)
            gram(head_at(place - step + 1, 1 - core))
            gram(head_at(place + step - 1, 1 - core))

        receive(1, step)
        gram(head_at(place - step, core))
        gram(head_at(place + step, core))
        return carry

    lax.fori_loop(1, depth, advance, 0)
    for direction, part in ((0, 0), (1, 1)):
        ring_arrival(direction, part, depth).wait_recv()
        pair(direction, part, depth, core).start()
    if depth > 1:
        pair_arrivals(depth - 1)
        gram(head_at(place - depth + 1, 1 - core))
        gram(head_at(place + depth - 1, 1 - core))
    gram_far(head_at(place - depth, core))
    for direction, part in ((0, 0), (1, 1)):
        pair(direction, part, depth, 1 - core).wait_recv()
    gram_far(head_at(place - depth, 1 - core))
    if lending:
        @pl.when(borrows)
        def _():
            for which in range(2):
                gram_for_mirror(which)

    def finish(order, carry):
        away = lax.div(order, 4)
        kind = lax.rem(order, 4)
        head = head_at(
            place + (away + 1) * (2 * lax.rem(kind, 2) - 1), lax.rem(core + lax.div(kind, 2), 2)
        )
        collect(head)
        return carry

    def collect(head):
        owner = lax.div(head, per_group)
        local = lax.rem(head, per_group)

        @pl.when(owner == me)
        def _():
            for shift in range(1, groups):
                sum_copy(shift, local).wait_recv()
            value = total[local]
            for shift in range(1, groups):
                value = value + arrived[shift - 1, local].astype(jnp.float32)
            total[local] = value * scale

    collect(here)
    collect(partner)
    lax.fori_loop(0, 4 * (depth - 1), finish, 0)
    collect(head_at(place - depth, core))
    collect(head_at(place - depth, 1 - core))

    def drain(head, carry):
        rows_copy(head).wait()
        owner = lax.div(head, per_group)
        local = lax.rem(head, per_group)
        shift = lax.rem(owner - me + groups, groups)

        sends = shift != 0
        if lending:
            lent_out = lends & (lax.div(head, 2) == (layers - 1 - level) * 2 + 1 - side)
            sends = sends & jnp.logical_not(lent_out)

        @pl.when(sends)
        def _():
            sum_copy(shift, local).wait_send()

        return carry

    lax.fori_loop(0, heads, drain, 0)

    def drain_sends(step, carry):
        for (direction, part), distance in reach.items():
            @pl.when(step < distance)
            def _():
                ring(direction, part, step).wait_send()

            @pl.when((step > 0) & (step <= distance))
            def _():
                pair(direction, part, step, core).wait_send()
        return carry

    lax.fori_loop(0, depth + 1, drain_sends, 0)
    for part in range(2):
        pair(0, part, 0, core).wait_send()
    if lending:
        @pl.when(borrows)
        def _():
            for which in range(2):
                lent_copy(which).wait_send()


def exchange(queries, keys, values, groups, heads):
    rows, cols = queries.shape
    per_group = heads // groups
    depth = heads // 4
    dma = pltpu.SemaphoreType.DMA
    vmem = pl.BlockSpec(memory_space=pltpu.VMEM)
    return pl.pallas_call(
        functools.partial(exchange_kernel, groups, heads, 2.0 / (rows * groups)),
        out_shape=(
            pltpu.VMEM((rows // heads, heads * cols), jnp.bfloat16),
            pltpu.VMEM((per_group, cols, cols), jnp.float32),
        ),
        in_specs=[pl.BlockSpec(memory_space=pltpu.HBM)] * 3,
        out_specs=(vmem, vmem),
        scratch_shapes=[
            pltpu.VMEM((rows, cols), jnp.bfloat16),
            pltpu.VMEM((rows, cols), jnp.bfloat16),
            pltpu.VMEM((rows, cols), jnp.bfloat16),
            pltpu.VMEM((heads, rows, cols), jnp.bfloat16),
            pltpu.VMEM((groups - 1, per_group, cols, cols), jnp.bfloat16),
            pltpu.VMEM((groups - 1, per_group, cols, cols), jnp.bfloat16),
            pltpu.VMEM((2, cols, cols), jnp.bfloat16),
            dma((2, 2, depth)),
            dma((2, 2, depth)),
            dma((2, 2, depth + 1)),
            dma((2, 2, depth + 1)),
            dma((groups - 1, per_group)),
            dma((groups - 1, per_group)),
            dma((heads,)),
            dma((3,)),
            dma((2,)),
        ],
        compiler_params=pltpu.CompilerParams(
            collective_id=0, has_side_effects=True, vmem_limit_bytes=109 * 512 * 1024
        ),
    )(queries, keys, values)


def body(queries, keys, values):
    cols = queries.shape[1]
    regrouped, total = exchange(
        queries, keys, values, lax.axis_size("dp"), lax.axis_size("head")
    )
    return (regrouped, total.reshape(-1, cols))


def solution(mesh):
    in_specs = (P("dp", "head"), P("dp", "head"), P("dp", "head"))
    out_specs = (P(("dp", "head"), None), P("dp", "head"))
    return jax.shard_map(body, mesh=mesh, in_specs=in_specs, out_specs=out_specs, check_vma=False)
```

```python
import functools
import math

import jax
import jax.numpy as jnp
from jax import lax
from jax.experimental import pallas as pl
from jax.experimental.pallas import tpu as pltpu
from jax.sharding import PartitionSpec as P

HEAD_SIZE = 128
MESH = pl.DeviceIdType.MESH


def exchange_kernel(
    groups, heads, scale,
    query_hbm, key_hbm, value_hbm, regrouped_ref, total,
    query_ref, key_ref, value_ref, gathered, leaving, arrived, lent, relayed,
    ring_send, ring_recv, pair_send, pair_recv, sum_send, sum_recv,
    rows_sem, load_sem, lent_send, lent_recv, relay_send,
):
    rows, cols = query_ref.shape
    half = rows // 2
    quarter = rows // 4
    chips = heads // 2
    depth = chips // 2
    per_group = heads // groups
    rows_out = rows // heads
    tile = min(cols, 256)
    me = lax.axis_index("dp")
    here = lax.axis_index("head")
    core = lax.rem(here, 2)
    chip = lax.div(here, 2)
    layers = chips // 2
    side = lax.rem(chip, 2)
    level = lax.div(chip, 2)
    place = level + side * (2 * layers - 1 - 2 * level)

    def head_at(position, which):
        spot = lax.rem(position + 2 * chips, chips)
        far = lax.div(spot, layers)
        height = spot + far * (2 * layers - 1 - 2 * spot)
        return (height * 2 + far) * 2 + which

    right = head_at(place + 1, core)
    left = head_at(place - 1, core)
    partner = here + 1 - 2 * core

    loads = [
        pltpu.make_async_copy(source, target, load_sem.at[n])
        for n, (source, target) in enumerate(
            ((query_hbm, query_ref), (key_hbm, key_ref), (value_hbm, value_ref))
        )
    ]
    for load in loads:
        load.start()
    lending = groups == 2
    lends = level == (layers - 1) * me
    borrows = level == (layers - 1) * (1 - me)
    mirror = ((layers - 1 - level) * 2 + side) * 2 + core

    barrier = pltpu.get_barrier_semaphore()
    if lending:
        pl.semaphore_signal(barrier, inc=1, device_id=(me, mirror), device_id_type=MESH)
    for other in (right, left, partner):
        pl.semaphore_signal(barrier, inc=1, device_id=(me, other), device_id_type=MESH)
    for shift in range(1, groups):
        pl.semaphore_signal(
            barrier, inc=1, device_id=(lax.rem(me + shift, groups), here), device_id_type=MESH
        )

    def attend(part):
        def head_of(index, carry):
            lanes = pl.ds(pl.multiple_of(index * HEAD_SIZE, HEAD_SIZE), HEAD_SIZE)
            for strip in range(2 * part, 2 * part + 2):
                seen = (strip + 1) * quarter
                here_rows = pl.ds(strip * quarter, quarter)
                logits = lax.dot_general(
                    query_ref[here_rows, lanes], key_ref[pl.ds(0, seen), lanes],
                    (((1,), (1,)), ((), ())), preferred_element_type=jnp.float32,
                ) * (1.0 / math.sqrt(HEAD_SIZE))
                row = lax.broadcasted_iota(jnp.int32, logits.shape, 0) + strip * quarter
                column = lax.broadcasted_iota(jnp.int32, logits.shape, 1)
                logits = jnp.where(row >= column, logits, -1e30)
                raised = jnp.exp(logits - jnp.max(logits, axis=-1, keepdims=True))
                weight = raised * (1.0 / jnp.sum(raised, axis=-1, keepdims=True))
                gathered[here, here_rows, lanes] = jnp.dot(
                    weight.astype(jnp.bfloat16), value_ref[pl.ds(0, seen), lanes],
                    preferred_element_type=jnp.float32,
                ).astype(jnp.bfloat16)
            return carry

        lax.fori_loop(0, cols // HEAD_SIZE, head_of, 0)

    def block(head, part):
        return gathered.at[head, pl.ds(part * half, half)]

    def ring(direction, part, step):
        source = head_at(place + step * (2 * direction - 1), core)
        ref = block(source, part)
        return pltpu.make_async_remote_copy(
            src_ref=ref, dst_ref=ref,
            send_sem=ring_send.at[direction, part, step],
            recv_sem=ring_recv.at[direction, part, step],
            device_id=(me, right if direction == 0 else left), device_id_type=MESH,
        )

    def ring_arrival(direction, part, step):
        source = head_at(place + step * (2 * direction - 1), core)
        ref = block(source, part)
        return pltpu.make_async_remote_copy(
            src_ref=ref, dst_ref=ref,
            send_sem=ring_send.at[direction, part, step - 1],
            recv_sem=ring_recv.at[direction, part, step - 1],
            device_id=(me, right if direction == 0 else left), device_id_type=MESH,
        )

    def pair(direction, part, step, which):
        ref = block(head_at(place + step * (2 * direction - 1), which), part)
        return pltpu.make_async_remote_copy(
            src_ref=ref, dst_ref=ref,
            send_sem=pair_send.at[direction, part, step],
            recv_sem=pair_recv.at[direction, part, step],
            device_id=(me, partner), device_id_type=MESH,
        )

    def sum_copy(shift, local):
        return pltpu.make_async_remote_copy(
            src_ref=leaving.at[shift - 1, local], dst_ref=arrived.at[shift - 1, local],
            send_sem=sum_send.at[shift - 1, local], recv_sem=sum_recv.at[shift - 1, local],
            device_id=(lax.rem(me + shift, groups), here), device_id_type=MESH,
        )

    def rows_copy(head):
        return pltpu.make_async_copy(
            gathered.at[head, pl.ds(pl.multiple_of(here * rows_out, rows_out), rows_out)],
            regrouped_ref.at[:, pl.ds(pl.multiple_of(head * cols, cols), cols)],
            rows_sem.at[head],
        )

    def gram(head):
        rows_copy(head).start()
        owner = lax.div(head, per_group)
        local = lax.rem(head, per_group)
        shift = lax.rem(owner - me + groups, groups)

        def one(t, carry):
            where = pl.ds(pl.multiple_of(t * tile, tile), tile)
            term = lax.dot_general(
                gathered[head, :, where], gathered[here],
                (((0,), (0,)), ((), ())), preferred_element_type=jnp.float32,
            )

            @pl.when(shift == 0)
            def _():
                total[local, where] = term

            @pl.when(shift != 0)
            def _():
                leaving[shift - 1, local, where] = term.astype(jnp.bfloat16)

            return carry

        lax.fori_loop(0, cols // tile, one, 0)

        @pl.when(shift != 0)
        def _():
            sum_copy(shift, local).start()

    def lent_copy(which):
        return pltpu.make_async_remote_copy(
            src_ref=lent.at[which], dst_ref=relayed.at[which],
            send_sem=lent_send.at[which], recv_sem=lent_recv.at[which],
            device_id=(1 - me, here), device_id_type=MESH,
        )

    def relay_copy(which):
        local = lax.rem((level * 2 + 1 - side) * 2 + which, per_group)
        return pltpu.make_async_remote_copy(
            src_ref=relayed.at[which], dst_ref=arrived.at[0, local],
            send_sem=relay_send.at[which], recv_sem=sum_recv.at[0, local],
            device_id=(me, mirror), device_id_type=MESH,
        )

    def gram_for_mirror(which):
        head = (level * 2 + 1 - side) * 2 + which

        def one(t, carry):
            where = pl.ds(pl.multiple_of(t * tile, tile), tile)
            lent[which, where] = lax.dot_general(
                gathered[head, :, where], gathered[mirror],
                (((0,), (0,)), ((), ())), preferred_element_type=jnp.float32,
            ).astype(jnp.bfloat16)
            return carry

        lax.fori_loop(0, cols // tile, one, 0)
        lent_copy(which).start()

    def gram_far(head):
        if not lending:
            gram(head)
            return

        @pl.when(lends)
        def _():
            rows_copy(head).start()

        @pl.when(jnp.logical_not(lends))
        def _():
            gram(head)

    reach = {(0, 0): depth, (1, 0): depth - 1, (0, 1): depth - 1, (1, 1): depth}
    for load in loads:
        load.wait()
    for part in range(2):
        attend(part)
        if part == 0:
            pl.semaphore_wait(barrier, 3 + groups - 1 + int(lending))
        for direction in range(2):
            ring(direction, part, 0).start()
        pair(0, part, 0, core).start()
    gram(here)

    def receive(part, step):
        for direction in range(2):
            ring_arrival(direction, part, step).wait_recv()
            if reach[direction, part] == depth:
                ring(direction, part, step).start()
            else:
                @pl.when(step < depth - 1)
                def _():
                    ring(direction, part, step).start()
            pair(direction, part, step, core).start()

    def pair_arrivals(step):
        for part in range(2):
            for direction in range(2):
                pair(direction, part, step, 1 - core).wait_recv()

    def advance(step, carry):
        receive(0, step)

        @pl.when(step == 1)
        def _():
            for part in range(2):
                pair(0, part, 0, 1 - core).wait_recv()
            gram(partner)

        @pl.when(step > 1)
        def _():
            pair_arrivals(step - 1)
            gram(head_at(place - step + 1, 1 - core))
            gram(head_at(place + step - 1, 1 - core))

        receive(1, step)
        gram(head_at(place - step, core))
        gram(head_at(place + step, core))
        return carry

    lax.fori_loop(1, depth, advance, 0)
    for direction, part in ((0, 0), (1, 1)):
        ring_arrival(direction, part, depth).wait_recv()
        pair(direction, part, depth, core).start()
    if depth > 1:
        pair_arrivals(depth - 1)
        gram(head_at(place - depth + 1, 1 - core))
        gram(head_at(place + depth - 1, 1 - core))
    gram_far(head_at(place - depth, core))
    for direction, part in ((0, 0), (1, 1)):
        pair(direction, part, depth, 1 - core).wait_recv()
    gram_far(head_at(place - depth, 1 - core))
    if lending:
        @pl.when(borrows)
        def _():
            for which in range(2):
                gram_for_mirror(which)

    def finish(order, carry):
        away = lax.div(order, 4)
        kind = lax.rem(order, 4)
        head = head_at(
            place + (away + 1) * (2 * lax.rem(kind, 2) - 1), lax.rem(core + lax.div(kind, 2), 2)
        )
        collect(head)
        return carry

    def collect(head):
        owner = lax.div(head, per_group)
        local = lax.rem(head, per_group)

        @pl.when(owner == me)
        def _():
            for shift in range(1, groups):
                sum_copy(shift, local).wait_recv()
            value = total[local]
            for shift in range(1, groups):
                value = value + arrived[shift - 1, local].astype(jnp.float32)
            total[local] = value * scale

    collect(here)
    collect(partner)
    lax.fori_loop(0, 4 * (depth - 1), finish, 0)
    collect(head_at(place - depth, core))
    collect(head_at(place - depth, 1 - core))

    if lending:
        @pl.when(lends)
        def _():
            for which in range(2):
                lent_copy(which).wait_recv()
                relay_copy(which).start()
            for which in range(2):
                relay_copy(which).wait_send()

    def drain(head, carry):
        rows_copy(head).wait()
        owner = lax.div(head, per_group)
        local = lax.rem(head, per_group)
        shift = lax.rem(owner - me + groups, groups)

        sends = shift != 0
        if lending:
            lent_out = lends & (lax.div(head, 2) == (layers - 1 - level) * 2 + 1 - side)
            sends = sends & jnp.logical_not(lent_out)

        @pl.when(sends)
        def _():
            sum_copy(shift, local).wait_send()

        return carry

    lax.fori_loop(0, heads, drain, 0)

    def drain_sends(step, carry):
        for (direction, part), distance in reach.items():
            @pl.when(step < distance)
            def _():
                ring(direction, part, step).wait_send()

            @pl.when((step > 0) & (step <= distance))
            def _():
                pair(direction, part, step, core).wait_send()
        return carry

    lax.fori_loop(0, depth + 1, drain_sends, 0)
    for part in range(2):
        pair(0, part, 0, core).wait_send()
    if lending:
        @pl.when(borrows)
        def _():
            for which in range(2):
                lent_copy(which).wait_send()


def exchange(queries, keys, values, groups, heads):
    rows, cols = queries.shape
    per_group = heads // groups
    depth = heads // 4
    dma = pltpu.SemaphoreType.DMA
    vmem = pl.BlockSpec(memory_space=pltpu.VMEM)
    return pl.pallas_call(
        functools.partial(exchange_kernel, groups, heads, 2.0 / (rows * groups)),
        out_shape=(
            pltpu.VMEM((rows // heads, heads * cols), jnp.bfloat16),
            pltpu.VMEM((per_group, cols, cols), jnp.float32),
        ),
        in_specs=[pl.BlockSpec(memory_space=pltpu.HBM)] * 3,
        out_specs=(vmem, vmem),
        scratch_shapes=[
            pltpu.VMEM((rows, cols), jnp.bfloat16),
            pltpu.VMEM((rows, cols), jnp.bfloat16),
            pltpu.VMEM((rows, cols), jnp.bfloat16),
            pltpu.VMEM((heads, rows, cols), jnp.bfloat16),
            pltpu.VMEM((groups - 1, per_group, cols, cols), jnp.bfloat16),
            pltpu.VMEM((groups - 1, per_group, cols, cols), jnp.bfloat16),
            pltpu.VMEM((2, cols, cols), jnp.bfloat16),
            pltpu.VMEM((2, cols, cols), jnp.bfloat16),
            dma((2, 2, depth)),
            dma((2, 2, depth)),
            dma((2, 2, depth + 1)),
            dma((2, 2, depth + 1)),
            dma((groups - 1, per_group)),
            dma((groups - 1, per_group)),
            dma((heads,)),
            dma((3,)),
            dma((2,)),
            dma((2,)),
            dma((2,)),
        ],
        compiler_params=pltpu.CompilerParams(
            collective_id=0, has_side_effects=True, vmem_limit_bytes=109 * 512 * 1024
        ),
    )(queries, keys, values)


def body(queries, keys, values):
    cols = queries.shape[1]
    regrouped, total = exchange(
        queries, keys, values, lax.axis_size("dp"), lax.axis_size("head")
    )
    return (regrouped, total.reshape(-1, cols))


def solution(mesh):
    in_specs = (P("dp", "head"), P("dp", "head"), P("dp", "head"))
    out_specs = (P(("dp", "head"), None), P("dp", "head"))
    return jax.shard_map(body, mesh=mesh, in_specs=in_specs, out_specs=out_specs, check_vma=False)
```

```python
import functools
import math

import jax
import jax.numpy as jnp
from jax import lax
from jax.experimental import pallas as pl
from jax.experimental.pallas import tpu as pltpu
from jax.sharding import PartitionSpec as P

HEAD_SIZE = 128
MESH = pl.DeviceIdType.MESH


def exchange_kernel(
    groups, heads, scale,
    query_hbm, key_hbm, value_hbm, regrouped_ref, total,
    query_ref, key_ref, value_ref, gathered, leaving, arrived, lent, relayed,
    ring_send, ring_recv, pair_send, pair_recv, sum_send, sum_recv,
    rows_sem, load_sem, lent_send, lent_recv, relay_send,
):
    rows, cols = query_ref.shape
    half = rows // 2
    quarter = rows // 4
    chips = heads // 2
    depth = chips // 2
    per_group = heads // groups
    rows_out = rows // heads
    tile = min(cols, 256)
    me = lax.axis_index("dp")
    here = lax.axis_index("head")
    core = lax.rem(here, 2)
    chip = lax.div(here, 2)
    layers = chips // 2
    side = lax.rem(chip, 2)
    level = lax.div(chip, 2)
    place = level + side * (2 * layers - 1 - 2 * level)

    def head_at(position, which):
        spot = lax.rem(position + 2 * chips, chips)
        far = lax.div(spot, layers)
        height = spot + far * (2 * layers - 1 - 2 * spot)
        return (height * 2 + far) * 2 + which

    right = head_at(place + 1, core)
    left = head_at(place - 1, core)
    partner = here + 1 - 2 * core

    loads = [
        pltpu.make_async_copy(source, target, load_sem.at[n])
        for n, (source, target) in enumerate(
            ((query_hbm, query_ref), (key_hbm, key_ref), (value_hbm, value_ref))
        )
    ]
    for load in loads:
        load.start()
    lending = groups == 2 and layers >= 4
    lends = level == (layers - 1) * me
    borrows = level == (layers - 1) * (1 - me)
    held = (level + 2 * me - 1) * 2 + 1 - side
    mirror = ((layers - 1 - level) * 2 + side) * 2 + core

    barrier = pltpu.get_barrier_semaphore()
    if lending:
        pl.semaphore_signal(barrier, inc=1, device_id=(me, mirror), device_id_type=MESH)
    for other in (right, left, partner):
        pl.semaphore_signal(barrier, inc=1, device_id=(me, other), device_id_type=MESH)
    for shift in range(1, groups):
        pl.semaphore_signal(
            barrier, inc=1, device_id=(lax.rem(me + shift, groups), here), device_id_type=MESH
        )

    def attend(part):
        def head_of(index, carry):
            lanes = pl.ds(pl.multiple_of(index * HEAD_SIZE, HEAD_SIZE), HEAD_SIZE)
            for strip in range(2 * part, 2 * part + 2):
                seen = (strip + 1) * quarter
                here_rows = pl.ds(strip * quarter, quarter)
                logits = lax.dot_general(
                    query_ref[here_rows, lanes], key_ref[pl.ds(0, seen), lanes],
                    (((1,), (1,)), ((), ())), preferred_element_type=jnp.float32,
                ) * (1.0 / math.sqrt(HEAD_SIZE))
                row = lax.broadcasted_iota(jnp.int32, logits.shape, 0) + strip * quarter
                column = lax.broadcasted_iota(jnp.int32, logits.shape, 1)
                logits = jnp.where(row >= column, logits, -1e30)
                raised = jnp.exp(logits - jnp.max(logits, axis=-1, keepdims=True))
                weight = raised * (1.0 / jnp.sum(raised, axis=-1, keepdims=True))
                gathered[here, here_rows, lanes] = jnp.dot(
                    weight.astype(jnp.bfloat16), value_ref[pl.ds(0, seen), lanes],
                    preferred_element_type=jnp.float32,
                ).astype(jnp.bfloat16)
            return carry

        lax.fori_loop(0, cols // HEAD_SIZE, head_of, 0)

    def block(head, part):
        return gathered.at[head, pl.ds(part * half, half)]

    def ring(direction, part, step):
        source = head_at(place + step * (2 * direction - 1), core)
        ref = block(source, part)
        return pltpu.make_async_remote_copy(
            src_ref=ref, dst_ref=ref,
            send_sem=ring_send.at[direction, part, step],
            recv_sem=ring_recv.at[direction, part, step],
            device_id=(me, right if direction == 0 else left), device_id_type=MESH,
        )

    def ring_arrival(direction, part, step):
        source = head_at(place + step * (2 * direction - 1), core)
        ref = block(source, part)
        return pltpu.make_async_remote_copy(
            src_ref=ref, dst_ref=ref,
            send_sem=ring_send.at[direction, part, step - 1],
            recv_sem=ring_recv.at[direction, part, step - 1],
            device_id=(me, right if direction == 0 else left), device_id_type=MESH,
        )

    def pair(direction, part, step, which):
        ref = block(head_at(place + step * (2 * direction - 1), which), part)
        return pltpu.make_async_remote_copy(
            src_ref=ref, dst_ref=ref,
            send_sem=pair_send.at[direction, part, step],
            recv_sem=pair_recv.at[direction, part, step],
            device_id=(me, partner), device_id_type=MESH,
        )

    def sum_copy(shift, local):
        return pltpu.make_async_remote_copy(
            src_ref=leaving.at[shift - 1, local], dst_ref=arrived.at[shift - 1, local],
            send_sem=sum_send.at[shift - 1, local], recv_sem=sum_recv.at[shift - 1, local],
            device_id=(lax.rem(me + shift, groups), here), device_id_type=MESH,
        )

    def rows_copy(head):
        return pltpu.make_async_copy(
            gathered.at[head, pl.ds(pl.multiple_of(here * rows_out, rows_out), rows_out)],
            regrouped_ref.at[:, pl.ds(pl.multiple_of(head * cols, cols), cols)],
            rows_sem.at[head],
        )

    def gram(head):
        rows_copy(head).start()
        owner = lax.div(head, per_group)
        local = lax.rem(head, per_group)
        shift = lax.rem(owner - me + groups, groups)

        def one(t, carry):
            where = pl.ds(pl.multiple_of(t * tile, tile), tile)
            term = lax.dot_general(
                gathered[head, :, where], gathered[here],
                (((0,), (0,)), ((), ())), preferred_element_type=jnp.float32,
            )

            @pl.when(shift == 0)
            def _():
                total[local, where] = term

            @pl.when(shift != 0)
            def _():
                leaving[shift - 1, local, where] = term.astype(jnp.bfloat16)

            return carry

        lax.fori_loop(0, cols // tile, one, 0)

        sends = shift != 0
        if lending:
            sends = sends & jnp.logical_not(borrows & (lax.div(head, 2) == held))

        @pl.when(sends)
        def _():
            sum_copy(shift, local).start()

    def lent_copy(which):
        return pltpu.make_async_remote_copy(
            src_ref=lent.at[which], dst_ref=relayed.at[which],
            send_sem=lent_send.at[which], recv_sem=lent_recv.at[which],
            device_id=(1 - me, here), device_id_type=MESH,
        )

    def relay_copy(which):
        local = lax.rem((level * 2 + 1 - side) * 2 + which, per_group)
        return pltpu.make_async_remote_copy(
            src_ref=relayed.at[which], dst_ref=arrived.at[0, local],
            send_sem=relay_send.at[which], recv_sem=sum_recv.at[0, local],
            device_id=(me, mirror), device_id_type=MESH,
        )

    def gram_for_mirror(which):
        head = (level * 2 + 1 - side) * 2 + which

        def one(t, carry):
            where = pl.ds(pl.multiple_of(t * tile, tile), tile)
            lent[which, where] = lax.dot_general(
                gathered[head, :, where], gathered[mirror],
                (((0,), (0,)), ((), ())), preferred_element_type=jnp.float32,
            ).astype(jnp.bfloat16)
            return carry

        lax.fori_loop(0, cols // tile, one, 0)
        lent_copy(which).start()

    def gram_far(head):
        if not lending:
            gram(head)
            return

        @pl.when(lends)
        def _():
            rows_copy(head).start()

        @pl.when(jnp.logical_not(lends))
        def _():
            gram(head)

    reach = {(0, 0): depth, (1, 0): depth - 1, (0, 1): depth - 1, (1, 1): depth}
    for load in loads:
        load.wait()
    for part in range(2):
        attend(part)
        if part == 0:
            pl.semaphore_wait(barrier, 3 + groups - 1 + int(lending))
        for direction in range(2):
            ring(direction, part, 0).start()
        pair(0, part, 0, core).start()
    gram(here)

    def receive(part, step):
        for direction in range(2):
            ring_arrival(direction, part, step).wait_recv()
            if reach[direction, part] == depth:
                ring(direction, part, step).start()
            else:
                @pl.when(step < depth - 1)
                def _():
                    ring(direction, part, step).start()
            pair(direction, part, step, core).start()

    def pair_arrivals(step):
        for part in range(2):
            for direction in range(2):
                pair(direction, part, step, 1 - core).wait_recv()

    def advance(step, carry):
        receive(0, step)

        @pl.when(step == 1)
        def _():
            for part in range(2):
                pair(0, part, 0, 1 - core).wait_recv()
            gram(partner)

        @pl.when(step > 1)
        def _():
            pair_arrivals(step - 1)
            gram(head_at(place - step + 1, 1 - core))
            gram(head_at(place + step - 1, 1 - core))

        receive(1, step)
        if lending:
            @pl.when(borrows & (step == depth - 1))
            def _():
                for which in range(2):
                    gram_for_mirror(which)
                for which in range(2):
                    sum_copy(1, lax.rem(held * 2 + which, per_group)).start()

        gram(head_at(place - step, core))
        gram(head_at(place + step, core))
        return carry

    lax.fori_loop(1, depth, advance, 0)
    for direction, part in ((0, 0), (1, 1)):
        ring_arrival(direction, part, depth).wait_recv()
        pair(direction, part, depth, core).start()
    if depth > 1:
        pair_arrivals(depth - 1)
        gram(head_at(place - depth + 1, 1 - core))
        gram(head_at(place + depth - 1, 1 - core))
    gram_far(head_at(place - depth, core))
    for direction, part in ((0, 0), (1, 1)):
        pair(direction, part, depth, 1 - core).wait_recv()
    gram_far(head_at(place - depth, 1 - core))

    def finish(order, carry):
        if lending:
            @pl.when(lends & (order == 4))
            def _():
                for which in range(2):
                    lent_copy(which).wait_recv()
                    relay_copy(which).start()

        away = lax.div(order, 4)
        kind = lax.rem(order, 4)
        head = head_at(
            place + (away + 1) * (2 * lax.rem(kind, 2) - 1), lax.rem(core + lax.div(kind, 2), 2)
        )
        collect(head)
        return carry

    def collect(head):
        owner = lax.div(head, per_group)
        local = lax.rem(head, per_group)

        @pl.when(owner == me)
        def _():
            for shift in range(1, groups):
                sum_copy(shift, local).wait_recv()
            value = total[local]
            for shift in range(1, groups):
                value = value + arrived[shift - 1, local].astype(jnp.float32)
            total[local] = value * scale

    collect(here)
    collect(partner)
    lax.fori_loop(0, 4 * (depth - 1), finish, 0)
    collect(head_at(place - depth, core))
    collect(head_at(place - depth, 1 - core))

    if lending:
        @pl.when(lends)
        def _():
            for which in range(2):
                relay_copy(which).wait_send()

    def drain(head, carry):
        rows_copy(head).wait()
        owner = lax.div(head, per_group)
        local = lax.rem(head, per_group)
        shift = lax.rem(owner - me + groups, groups)

        sends = shift != 0
        if lending:
            lent_out = lends & (lax.div(head, 2) == (layers - 1 - level) * 2 + 1 - side)
            sends = sends & jnp.logical_not(lent_out)

        @pl.when(sends)
        def _():
            sum_copy(shift, local).wait_send()

        return carry

    lax.fori_loop(0, heads, drain, 0)

    def drain_sends(step, carry):
        for (direction, part), distance in reach.items():
            @pl.when(step < distance)
            def _():
                ring(direction, part, step).wait_send()

            @pl.when((step > 0) & (step <= distance))
            def _():
                pair(direction, part, step, core).wait_send()
        return carry

    lax.fori_loop(0, depth + 1, drain_sends, 0)
    for part in range(2):
        pair(0, part, 0, core).wait_send()
    if lending:
        @pl.when(borrows)
        def _():
            for which in range(2):
                lent_copy(which).wait_send()


def exchange(queries, keys, values, groups, heads):
    rows, cols = queries.shape
    per_group = heads // groups
    depth = heads // 4
    dma = pltpu.SemaphoreType.DMA
    vmem = pl.BlockSpec(memory_space=pltpu.VMEM)
    return pl.pallas_call(
        functools.partial(exchange_kernel, groups, heads, 2.0 / (rows * groups)),
        out_shape=(
            pltpu.VMEM((rows // heads, heads * cols), jnp.bfloat16),
            pltpu.VMEM((per_group, cols, cols), jnp.float32),
        ),
        in_specs=[pl.BlockSpec(memory_space=pltpu.HBM)] * 3,
        out_specs=(vmem, vmem),
        scratch_shapes=[
            pltpu.VMEM((rows, cols), jnp.bfloat16),
            pltpu.VMEM((rows, cols), jnp.bfloat16),
            pltpu.VMEM((rows, cols), jnp.bfloat16),
            pltpu.VMEM((heads, rows, cols), jnp.bfloat16),
            pltpu.VMEM((groups - 1, per_group, cols, cols), jnp.bfloat16),
            pltpu.VMEM((groups - 1, per_group, cols, cols), jnp.bfloat16),
            pltpu.VMEM((2, cols, cols), jnp.bfloat16),
            pltpu.VMEM((2, cols, cols), jnp.bfloat16),
            dma((2, 2, depth)),
            dma((2, 2, depth)),
            dma((2, 2, depth + 1)),
            dma((2, 2, depth + 1)),
            dma((groups - 1, per_group)),
            dma((groups - 1, per_group)),
            dma((heads,)),
            dma((3,)),
            dma((2,)),
            dma((2,)),
            dma((2,)),
        ],
        compiler_params=pltpu.CompilerParams(
            collective_id=0, has_side_effects=True, vmem_limit_bytes=109 * 512 * 1024
        ),
    )(queries, keys, values)


def body(queries, keys, values):
    cols = queries.shape[1]
    regrouped, total = exchange(
        queries, keys, values, lax.axis_size("dp"), lax.axis_size("head")
    )
    return (regrouped, total.reshape(-1, cols))


def solution(mesh):
    in_specs = (P("dp", "head"), P("dp", "head"), P("dp", "head"))
    out_specs = (P(("dp", "head"), None), P("dp", "head"))
    return jax.shard_map(body, mesh=mesh, in_specs=in_specs, out_specs=out_specs, check_vma=False)
```
